32 devices in a mesh: lat: 8 (over z, y), grp: 4 (over x, core).
Axes of the slice: x: 2, y: 2, z: 4, core: 2. Of those that a mesh axis runs over, the one named last changes fastest.
Arguments:
- tokens: bfloat16 [384, 64, 1024], P('grp', 'lat'), may hold values from -6 to 6
- cotangent: bfloat16 [384, 64, 1024], P('grp', 'lat'), may hold values from -6 to 6
- gain: float32 [384], P('grp'), may hold values from 0.5 to 1.5
- shift: float32 [384], P('grp'), may hold values from -3 to 3
- w_in: float32 [4, 2, 96, 96], P('grp'), may hold values from -0.4375 to 0.4375
- b_in: float32 [4, 2, 96], P('grp'), may hold values from -0.3 to 0.3
- w_out: float32 [4, 2, 96, 96], P('grp'), may hold values from -0.4375 to 0.4375
- b_out: float32 [4, 2, 96], P('grp'), may hold values from -0.12 to 0.12
Outputs:
- mixed: bfloat16 [384, 64, 1024], P('grp', 'lat')
- grad_tokens: bfloat16 [384, 64, 1024], P('grp', 'lat')
- grad_weights: float32 [4, 36864], P('grp', 'lat')
The draws below stay inside these ranges and needn't reach their ends.
All inputs are finite; a program needn't handle non-finite values.
Results may differ from the reference program's by a relative error of at most 0.012.
Values sent between devices are 32-bit elements; how exact they have to be, the bound alone decides.
A program may use at most 128 MiB of HBM per device.

```python
import math
import jax
import jax.numpy as jnp
from jax import lax

BLOCK_SIZE = 96
LON = 1024
LAT_ROWS = 64
MODES = 512
BLOCKS = 4
WIDTH = 384


def block_levels(rng, dims, shards, low, high):
    factor_of = 1.0
    for axis_at, shards_of in shards:
        draws = jax.random.uniform(jax.random.fold_in(jax.random.fold_in(rng, 6), axis_at), (shards_of,), jnp.float32, low / len(shards), high / len(shards))
        factor_of = factor_of * jnp.repeat(jnp.exp(draws), dims[axis_at] // shards_of).reshape((-1,) + (1,) * (len(dims) - 1 - axis_at))
    return factor_of


def centred(own_key, dims, scale, limit, cuts=(), held_as=jnp.bfloat16):
    level = block_levels(own_key, dims, cuts, -0.22, 0.18) if cuts else 1.0
    values = jax.random.normal(own_key, dims, jnp.float32) * scale * level
    return jnp.minimum(jnp.maximum(values, -limit), limit).astype(held_as)


def setup_inputs(seed: int = 0) -> dict:
    streams_of = jax.random.split(jax.random.key(seed), 9)
    return {
        "tokens": centred(streams_of[0], (WIDTH, LAT_ROWS, LON), 1.0, 6.0, ((0, 4), (1, 8))),
        "cotangent": centred(streams_of[1], (WIDTH, LAT_ROWS, LON), 1.0, 6.0, ((0, 4), (1, 8))),
        "gain": jnp.clip(1.0 + 0.1 * jax.random.normal(streams_of[2], (WIDTH,), jnp.float32), 0.5, 1.5),
        "shift": centred(streams_of[3], (WIDTH,), 0.5, 3.0, ((0, 4),), jnp.float32),
        "w_in": centred(streams_of[4], (BLOCKS, 2, BLOCK_SIZE, BLOCK_SIZE), (2 * BLOCK_SIZE) ** -0.5, 0.4375, ((0, 4),), jnp.float32),
        "b_in": centred(streams_of[5], (BLOCKS, 2, BLOCK_SIZE), 0.05, 0.3, ((0, 4),), jnp.float32),
        "w_out": centred(streams_of[6], (BLOCKS, 2, BLOCK_SIZE, BLOCK_SIZE), (2 * BLOCK_SIZE) ** -0.5, 0.4375, ((0, 4),), jnp.float32),
        "b_out": centred(streams_of[7], (BLOCKS, 2, BLOCK_SIZE), 0.02, 0.12, ((0, 4),), jnp.float32),
    }


highest = lax.Precision.HIGHEST
shrink_level = 0.01
norm_eps = 1e-05

def complex_mix(left_real, left_imag, w_real, w_imag):
    form = 'ihk,io->ohk'
    out_real = jnp.einsum(form, left_real, w_real, precision=highest) - jnp.einsum(form, left_imag, w_imag, precision=highest)
    out_imag = jnp.einsum(form, left_imag, w_real, precision=highest) + jnp.einsum(form, left_real, w_imag, precision=highest)
    return (out_real, out_imag)

def shrink(value):
    return jnp.sign(value) * jnp.maximum(jnp.abs(value) - shrink_level, 0.0)

def spectral_filter(field, in_real, in_imag, out_real, out_imag, bias_in, bias_out):
    half = jnp.fft.rfft(field, axis=2, norm='ortho')[:, :, :MODES]
    spectrum = jnp.fft.fft(half, axis=1, norm='ortho')
    pre_real, pre_imag = complex_mix(jnp.real(spectrum), jnp.imag(spectrum), in_real, in_imag)
    act_real = jax.nn.relu(pre_real + bias_in[0][:, None, None])
    act_imag = jax.nn.relu(pre_imag + bias_in[1][:, None, None])
    post_real, post_imag = complex_mix(act_real, act_imag, out_real, out_imag)
    shrunk_real = shrink(post_real + bias_out[0][:, None, None])
    shrunk_imag = shrink(post_imag + bias_out[1][:, None, None])
    back = jnp.fft.ifft(lax.complex(shrunk_real, shrunk_imag), axis=1, norm='ortho')
    return jnp.fft.irfft(back, n=LON, axis=2, norm='ortho')

def per_block(items):
    field, grad_part, block_in, bias_in, block_out, bias_out = items

    def apply_filter(value, in_real, in_imag, out_real, out_imag):
        return spectral_filter(value, in_real, in_imag, out_real, out_imag, bias_in, bias_out)
    filtered, pullback = jax.vjp(apply_filter, field, block_in[0], block_in[1], block_out[0], block_out[1])
    d_field, g_in_real, g_in_imag, g_out_real, g_out_imag = pullback(grad_part)
    grads = jnp.stack([g_in_real, g_in_imag, g_out_real, g_out_imag]).reshape(-1)
    return (filtered, d_field, grads)

def reference(tokens, cotangent, gain, shift, w_in, b_in, w_out, b_out):
    tok_val = tokens.astype(jnp.float32)
    grad_val = cotangent.astype(jnp.float32)
    token_mean = lax.optimization_barrier(jnp.mean(tok_val, axis=0))
    square_mean = lax.optimization_barrier(jnp.mean(tok_val * tok_val, axis=0))
    inv_std = lax.rsqrt(square_mean - token_mean * token_mean + norm_eps)
    normed = (tok_val - token_mean) * inv_std
    normal_out = normed * gain[:, None, None] + shift[:, None, None]

    def shaped(value):
        return value.reshape(BLOCKS, BLOCK_SIZE, LAT_ROWS, LON)
    filtered, d_filter, grads = lax.map(per_block, (shaped(normal_out), shaped(grad_val), w_in, b_in, w_out, b_out))
    filtered = filtered.reshape(WIDTH, LAT_ROWS, LON)
    d_filter = d_filter.reshape(WIDTH, LAT_ROWS, LON)
    mixed = (filtered + normal_out + tok_val).astype(jnp.bfloat16)
    d_normal = grad_val + d_filter
    dnorm = d_normal * gain[:, None, None]
    back_one = lax.optimization_barrier(jnp.mean(dnorm, axis=0))
    back_two = lax.optimization_barrier(jnp.mean(dnorm * normed, axis=0))
    grad_tokens = (grad_val + inv_std * (dnorm - back_one - normed * back_two)).astype(jnp.bfloat16)
    grad_weights = grads * (1.0 / math.sqrt(LAT_ROWS * MODES))
    return (mixed, grad_tokens, grad_weights)
```

```python
import math

import numpy as np
import jax
import jax.numpy as jnp
from jax import lax
from jax.sharding import PartitionSpec as P

shrink_level = 0.01
norm_eps = 1e-05


precise = lax.Precision.HIGH


def contract(form, left, right):
    return jnp.einsum(form, left, right, precision=precise, preferred_element_type=jnp.float32)


def angles(left_count, right_count, length):
    phase = np.arange(left_count)[:, None] * np.arange(right_count)[None, :] % length
    theta = phase * (2.0 * math.pi / length)
    return np.cos(theta), np.sin(theta)


def lon_table(length, modes, owners):
    cos_tab, sin_tab = angles(length, modes, length)
    both = np.stack([cos_tab, -sin_tab]) / math.sqrt(length)
    both = both.reshape(2, length, owners, modes // owners)
    return both.transpose(1, 2, 0, 3).astype(np.float32)


def lat_table(length):
    cos_tab, sin_tab = angles(length, length, length)
    table = np.stack([np.stack([cos_tab, -sin_tab]), np.stack([sin_tab, cos_tab])])
    return (table / math.sqrt(length)).transpose(2, 0, 3, 1).astype(np.float32)


def group_sum(value, name):
    count = lax.axis_size(name)
    total = value
    for step in range(1, count):
        pairs = [(at, (at + step) % count) for at in range(count)]
        total = total + lax.ppermute(value, name, pairs)
    return total


def swap(value):
    return lax.all_to_all(value, "lat", split_axis=0, concat_axis=0, tiled=True)


def mix_matrix(weight):
    real_part, imag_part = weight[0], weight[1]
    top = jnp.stack([real_part, imag_part], axis=1)
    low = jnp.stack([-imag_part, real_part], axis=1)
    return jnp.stack([top, low])


def shrink(value):
    return jnp.sign(value) * jnp.maximum(jnp.abs(value) - shrink_level, 0.0)


def matrix_grad(full):
    real_part = full[0, :, 0] + full[1, :, 1]
    imag_part = full[0, :, 1] - full[1, :, 0]
    return real_part, imag_part


def per_device(tokens, cotangent, gain, shift, w_in, b_in, w_out, b_out):
    chans, rows, length = tokens.shape
    lat_count = lax.axis_size("lat")
    all_chans = chans * lax.axis_size("grp")
    modes = length // 2
    own = modes // lat_count
    lat_len = rows * lat_count
    table = lon_table(length, modes, lat_count).reshape(length, 2 * modes)
    table = jnp.asarray(table)
    lat_tab = jnp.asarray(lat_table(lat_len)).reshape(lat_count, rows, 2, lat_len, 2)
    tok_val = tokens.astype(jnp.float32)
    grad_val = cotangent.astype(jnp.float32)

    def lon_send(field):
        out = jnp.einsum("crn,ndq->dcrq", field, table.reshape(length, lat_count, 2 * own),
                         precision=precise, preferred_element_type=jnp.float32)
        return swap(out.reshape(lat_count, chans * rows, 2 * own))

    def lat_in(parts):
        parts = parts.reshape(lat_count, chans, rows, 2, own)
        return contract("scrim,srikj->kmjc", parts, lat_tab)

    def lat_out(value):
        out = contract("kmjc,srikj->scrim", value, lat_tab)
        return swap(out.reshape(lat_count, chans * rows, 2 * own))

    def lon_back(parts):
        parts = parts.reshape(lat_count, chans, rows, 2 * own)
        return contract("dcrq,ndq->crn", parts, table.reshape(length, lat_count, 2 * own))

    sums = jnp.stack([jnp.sum(tok_val, axis=0), jnp.sum(tok_val * tok_val, axis=0)])
    sums = group_sum(sums, "grp")
    token_mean = sums[0] / all_chans
    inv_std = lax.rsqrt(sums[1] / all_chans - token_mean * token_mean + norm_eps)
    normed = (tok_val - token_mean) * inv_std
    normal_out = normed * gain[:, None, None] + shift[:, None, None]
    recv_field = lon_send(normal_out)
    recv_grad = lon_send(grad_val)

    mat_in, mat_out = mix_matrix(w_in[0]), mix_matrix(w_out[0])
    at_mode = lax.axis_index("lat") * own + jnp.arange(own)
    mode_weight = jnp.where(at_mode == 0, 1.0, 2.0).astype(jnp.float32)[None, :, None, None]
    spec = lat_in(recv_field)
    pre = contract("kmic,icjo->kmjo", spec, mat_in) + b_in[0]
    act = jax.nn.relu(pre)
    post = contract("kmic,icjo->kmjo", act, mat_out) + b_out[0]
    rows_field = lat_out(shrink(post) * mode_weight)

    grad = lat_in(recv_grad) * mode_weight
    d_post = jnp.where(jnp.abs(post) > shrink_level, grad, 0.0)
    d_act = contract("kmjo,icjo->kmic", d_post, mat_out)
    d_pre = jnp.where(pre > 0.0, d_act, 0.0)
    d_spec = contract("kmjo,icjo->kmic", d_pre, mat_in)
    rows_grad = lat_out(d_spec)
    full_out = contract("kmic,kmjo->icjo", act, d_post)
    full_in = contract("kmic,kmjo->icjo", spec, d_pre)
    grads = jnp.stack([*matrix_grad(full_in), *matrix_grad(full_out)])
    grads = grads.reshape(lat_count, -1) * (1.0 / math.sqrt(lat_len * modes))
    grad_weights = jnp.sum(swap(grads), axis=0, keepdims=True)

    mixed = (lon_back(rows_field) + normal_out + tok_val).astype(jnp.bfloat16)
    dnorm = (grad_val + lon_back(rows_grad)) * gain[:, None, None]
    back = group_sum(jnp.stack([jnp.sum(dnorm, axis=0), jnp.sum(dnorm * normed, axis=0)]), "grp")
    grad_tokens = grad_val + inv_std * (
        dnorm - back[0] / all_chans - normed * (back[1] / all_chans)
    )
    return (mixed, grad_tokens.astype(jnp.bfloat16), grad_weights)


def solution(mesh):
    in_specs = (
        P("grp", "lat", None),
        P("grp", "lat", None),
        P("grp"),
        P("grp"),
        P("grp", None, None, None),
        P("grp", None, None),
        P("grp", None, None, None),
        P("grp", None, None),
    )
    out_specs = (P("grp", "lat", None), P("grp", "lat", None), P("grp", "lat"))
    return jax.shard_map(
        per_device, mesh=mesh, in_specs=in_specs, out_specs=out_specs, check_vma=False
    )
```

```python
import math

import numpy as np
import jax
import jax.numpy as jnp
from jax import lax
from jax.sharding import PartitionSpec as P

shrink_level = 0.01
norm_eps = 1e-05


precise = lax.Precision.HIGH
exact = lax.Precision.HIGHEST


def contract(form, left, right, level=precise):
    return jnp.einsum(form, left, right, precision=level, preferred_element_type=jnp.float32)


def angles(left_count, right_count, length):
    phase = np.arange(left_count)[:, None] * np.arange(right_count)[None, :] % length
    theta = phase * (2.0 * math.pi / length)
    return np.cos(theta), np.sin(theta)


def lon_table(length, modes, owners):
    cos_tab, sin_tab = angles(length, modes, length)
    both = np.stack([cos_tab, -sin_tab]) / math.sqrt(length)
    both = both.reshape(2, length, owners, modes // owners)
    return both.transpose(1, 2, 0, 3).astype(np.float32)


def lat_table(length):
    cos_tab, sin_tab = angles(length, length, length)
    table = np.stack([np.stack([cos_tab, -sin_tab]), np.stack([sin_tab, cos_tab])])
    return (table / math.sqrt(length)).transpose(2, 0, 3, 1).astype(np.float32)


def group_sum(value, name):
    count = lax.axis_size(name)
    total = value
    for step in range(1, count):
        pairs = [(at, (at + step) % count) for at in range(count)]
        total = total + lax.ppermute(value, name, pairs)
    return total


def scatter_sum(pieces, name):
    count = lax.axis_size(name)
    own = lax.axis_index(name)
    total = lax.dynamic_slice_in_dim(pieces, own, 1, axis=0)
    for step in range(1, count):
        pairs = [(at, (at + step) % count) for at in range(count)]
        piece = lax.dynamic_slice_in_dim(pieces, (own + step) % count, 1, axis=0)
        total = total + lax.ppermute(piece, name, pairs)
    return total


def swap(value):
    return lax.all_to_all(value, "lat", split_axis=0, concat_axis=0, tiled=True)


def mix_matrix(weight):
    real_part, imag_part = weight[0], weight[1]
    top = jnp.stack([real_part, imag_part], axis=1)
    low = jnp.stack([-imag_part, real_part], axis=1)
    return jnp.stack([top, low])


def shrink(value):
    return jnp.sign(value) * jnp.maximum(jnp.abs(value) - shrink_level, 0.0)


def matrix_grad(full):
    real_part = full[0, :, 0] + full[1, :, 1]
    imag_part = full[0, :, 1] - full[1, :, 0]
    return real_part, imag_part


def per_device(tokens, cotangent, gain, shift, w_in, b_in, w_out, b_out):
    chans, rows, length = tokens.shape
    lat_count = lax.axis_size("lat")
    all_chans = chans * lax.axis_size("grp")
    modes = length // 2
    own = modes // lat_count
    lat_len = rows * lat_count
    table = lon_table(length, modes, lat_count).reshape(length, 2 * modes)
    table = jnp.asarray(table)
    lat_tab = jnp.asarray(lat_table(lat_len)).reshape(lat_count, rows, 2, lat_len, 2)
    tok_val = tokens.astype(jnp.float32)
    grad_val = cotangent.astype(jnp.float32)

    def lon_parts(field, level):
        out = contract("crn,ndq->dcrq", field, table.reshape(length, lat_count, 2 * own), level)
        return out.reshape(lat_count, chans * rows, 2 * own)

    def lat_in(parts, level):
        parts = parts.reshape(lat_count, chans, rows, 2, own)
        return contract("scrim,srikj->kmjc", parts, lat_tab, level)

    def lat_out(value):
        out = contract("kmjc,srikj->scrim", value, lat_tab)
        return out.reshape(lat_count, chans * rows, 2 * own)

    def lon_back(parts):
        parts = parts.reshape(lat_count, chans, rows, 2 * own)
        return contract("dcrq,ndq->crn", parts, table.reshape(length, lat_count, 2 * own))

    sums = jnp.stack([jnp.sum(tok_val, axis=0), jnp.sum(tok_val * tok_val, axis=0)])
    sums = group_sum(sums, "grp")
    token_mean = sums[0] / all_chans
    inv_std = lax.rsqrt(sums[1] / all_chans - token_mean * token_mean + norm_eps)
    normed = (tok_val - token_mean) * inv_std
    normal_out = normed * gain[:, None, None] + shift[:, None, None]
    send_field, grad_val = lax.optimization_barrier((lon_parts(normal_out, exact), grad_val))
    recv_field = swap(send_field)
    recv_grad = swap(lon_parts(grad_val, precise))

    mat_in, mat_out = mix_matrix(w_in[0]), mix_matrix(w_out[0])
    at_mode = lax.axis_index("lat") * own + jnp.arange(own)
    mode_weight = jnp.where(at_mode == 0, 1.0, 2.0).astype(jnp.float32)[None, :, None, None]
    spec = lat_in(recv_field, exact)
    pre = contract("kmic,icjo->kmjo", spec, mat_in, exact) + b_in[0]
    act = jax.nn.relu(pre)
    post = contract("kmic,icjo->kmjo", act, mat_out, exact) + b_out[0]
    back_field = lat_out(shrink(post) * mode_weight)
    back_field, spec, pre, act, post, recv_grad = lax.optimization_barrier(
        (back_field, spec, pre, act, post, recv_grad)
    )
    rows_field = swap(back_field)

    grad = lat_in(recv_grad, precise) * mode_weight
    d_post = jnp.where(jnp.abs(post) > shrink_level, grad, 0.0)
    d_act = contract("kmjo,icjo->kmic", d_post, mat_out)
    d_pre = jnp.where(pre > 0.0, d_act, 0.0)
    d_spec = contract("kmjo,icjo->kmic", d_pre, mat_in)
    back_grad, spec, act, d_post, d_pre = lax.optimization_barrier(
        (lat_out(d_spec), spec, act, d_post, d_pre)
    )
    rows_grad = swap(back_grad)
    full_out = contract("kmic,kmjo->icjo", act, d_post)
    full_in = contract("kmic,kmjo->icjo", spec, d_pre)
    grads = jnp.stack([*matrix_grad(full_in), *matrix_grad(full_out)])
    grads = grads.reshape(lat_count, -1) * (1.0 / math.sqrt(lat_len * modes))
    grad_weights = scatter_sum(grads, "lat")

    mixed = (lon_back(rows_field) + normal_out + tok_val).astype(jnp.bfloat16)
    dnorm = (grad_val + lon_back(rows_grad)) * gain[:, None, None]
    back = group_sum(jnp.stack([jnp.sum(dnorm, axis=0), jnp.sum(dnorm * normed, axis=0)]), "grp")
    grad_tokens = grad_val + inv_std * (
        dnorm - back[0] / all_chans - normed * (back[1] / all_chans)
    )
    return (mixed, grad_tokens.astype(jnp.bfloat16), grad_weights)


def solution(mesh):
    in_specs = (
        P("grp", "lat", None),
        P("grp", "lat", None),
        P("grp"),
        P("grp"),
        P("grp", None, None, None),
        P("grp", None, None),
        P("grp", None, None, None),
        P("grp", None, None),
    )
    out_specs = (P("grp", "lat", None), P("grp", "lat", None), P("grp", "lat"))
    return jax.shard_map(
        per_device, mesh=mesh, in_specs=in_specs, out_specs=out_specs, check_vma=False
    )
```
